32 devices in a mesh: dp: 4 (over y, x), seq: 8 (over z, core).
Axes of the slice: x: 2, y: 2, z: 4, core: 2. Of those that a mesh axis runs over, the one named last changes fastest.
Arguments:
- student_x: bfloat16 [4096, 4096], P(('dp', 'seq')), parts along dimension 0, may hold values from -60 to 60
- student_z: bfloat16 [4096, 4096], P(('dp', 'seq')), parts along dimension 0, may hold values from -6 to 6
- student_b: bfloat16 [4096, 1024], P(('dp', 'seq')), parts along dimension 0, may hold values from -0.5 to 0.5
- student_c: bfloat16 [4096, 1024], P(('dp', 'seq')), parts along dimension 0, may hold values from -6 to 6
- step_size: float32 [64, 4096], P(None, ('dp', 'seq')), parts along dimension 1, may hold values from 0 to 1
- decay_rate: float32 [64], replicated, may hold values from 0.5 to 2
- norm_gain: float32 [4096], replicated, may hold values from 0.5 to 1.5
- teacher_q: bfloat16 [4096, 4096], P(('dp', 'seq')), parts along dimension 0, may hold values from -140 to 140
- teacher_k: bfloat16 [4096, 1024], P(('dp', 'seq')), parts along dimension 0, may hold values from -7 to 7
- teacher_v: bfloat16 [4096, 1024], P(('dp', 'seq')), parts along dimension 0, may hold values from -6 to 6
Outputs:
- student_out: bfloat16 [4096, 4096], P(('dp', 'seq')), parts along dimension 0
- teacher_out: bfloat16 [4096, 4096], P(('dp', 'seq')), parts along dimension 0
The draws below stay inside these ranges and needn't reach their ends.
There are 4 independent parts, one for each index of `dp`. The reference program is written for one: setup_inputs(seed, part) draws one part's arguments, and reference() takes and returns one part's arrays. A program takes and returns all parts, laid end to end along the dimension named above; an argument that names none is the same for every part. Nothing has to cross between parts.
All inputs are finite; a program needn't handle non-finite values.
Results may differ from the reference program's by a relative error of at most 0.0075.
Values may be sent and summed in bfloat16 or wider, within the bound.
A program may use at most 256 MiB of HBM per device.

```python
import math
import jax
import jax.numpy as jnp
from jax import lax

LEARNER_COUNT = 64
HEAD_DIM = 64
STATE = 128
GROUPS = 8
Q_HEADS = 32
KV_HEADS = 8
HEAD_SIZE = 128
BLOCK = 128
TOK_DEV = 128
EXAMPLE_SPAN = 1024


def draw_student_x(key, part):
    key_base = jax.random.fold_in(key, 3)
    key_cols = jax.random.fold_in(key, 4)
    key_rows = jax.random.fold_in(key, 5)
    width = LEARNER_COUNT * HEAD_DIM
    starting_figure = jnp.clip(jax.random.normal(key_base, (EXAMPLE_SPAN, width), jnp.float32), -6.0, 6.0)
    columns = jnp.exp(jax.random.uniform(key_cols, (1, width), jnp.float32, 0.0, math.log(10.0)))
    rows = jnp.exp(jax.random.uniform(key_rows, (EXAMPLE_SPAN, 1), jnp.float32, 0.0, math.log(10.0)))
    return (starting_figure * columns * rows / 10.0).astype(jnp.bfloat16)


def draw_step_size(key, part):
    key_kind = jax.random.fold_in(key, 21)
    key_fast = jax.random.fold_in(key, 22)
    key_slow = jax.random.fold_in(key, 23)
    key_device = jax.random.fold_in(key, 24)
    key_rough = jax.random.fold_in(key, 25)
    lookup_tile_span = jax.random.fold_in(key, 26)
    key_amount = jax.random.fold_in(key, 27)
    fast_share = 0.5
    is_fast = jax.random.bernoulli(key_kind, fast_share, (LEARNER_COUNT, 1))
    fast_rate = jnp.exp(jax.random.uniform(key_fast, (LEARNER_COUNT, 1), jnp.float32, math.log(0.02), math.log(0.05)))
    slow_rate = jnp.exp(jax.random.uniform(key_slow, (LEARNER_COUNT, 1), jnp.float32, math.log(0.1), math.log(0.5))) / EXAMPLE_SPAN
    starting_figure = jnp.where(is_fast, fast_rate, slow_rate)
    segments = EXAMPLE_SPAN // TOK_DEV
    processor_factor = jnp.exp(jax.random.uniform(key_device, (LEARNER_COUNT, segments, 1), jnp.float32, math.log(0.5), math.log(2.0)))
    processor_factor = jnp.broadcast_to(processor_factor, (LEARNER_COUNT, segments, TOK_DEV)).reshape(LEARNER_COUNT, EXAMPLE_SPAN)
    approximate_guess = jax.random.uniform(key_rough, (LEARNER_COUNT, EXAMPLE_SPAN), jnp.float32, 0.5, 1.5)
    tile_groupings = jax.random.bernoulli(lookup_tile_span, 4.0 / EXAMPLE_SPAN, (LEARNER_COUNT, EXAMPLE_SPAN)).astype(jnp.float32)
    position_total = jax.random.uniform(key_amount, (LEARNER_COUNT, EXAMPLE_SPAN), jnp.float32, 0.25, 0.6)
    return starting_figure * processor_factor * approximate_guess + tile_groupings * position_total


def teacher_pair(key):
    key_query = jax.random.fold_in(key, 11)
    key_keys = jax.random.fold_in(key, 12)
    keys_flat = jnp.clip(jax.random.normal(key_keys, (EXAMPLE_SPAN, KV_HEADS * HEAD_SIZE), jnp.float32), -6.0, 6.0)
    queries = jnp.clip(jax.random.normal(key_query, (EXAMPLE_SPAN, Q_HEADS * HEAD_SIZE), jnp.float32), -6.0, 6.0)
    return (queries, keys_flat)


def draw_teacher_q(key, part):
    return teacher_pair(key)[0].astype(jnp.bfloat16)


def draw_teacher_k(key, part):
    return teacher_pair(key)[1].astype(jnp.bfloat16)


def level_of(rng, shape, pieces, smallest, top_value):
    def one(axis_at, parts):
        steps = jax.random.uniform(jax.random.fold_in(jax.random.fold_in(rng, 6), axis_at), (parts,), jnp.float32, smallest / len(pieces), top_value / len(pieces))
        return jnp.repeat(jnp.exp(steps), shape[axis_at] // parts).reshape((-1,) + (1,) * (len(shape) - axis_at - 1))

    gain = one(*pieces[0])
    for cut in pieces[1:]:
        gain = gain * one(*cut)
    return gain


def normal_values(stream_key, shape, scale, most, cuts=(), kind=jnp.bfloat16):
    entries = scale * jax.random.normal(stream_key, shape, jnp.float32)
    if cuts:
        entries = entries * level_of(stream_key, shape, cuts, -0.22, 0.18)
    return jnp.clip(entries, -most, most).astype(kind)


def setup_inputs(seed: int = 0, part: int = 0) -> dict:
    seeds = jax.random.split(jax.random.key(seed), 11)
    own_keys = jax.random.split(jax.random.fold_in(seeds[10], part), 11)
    student_x = draw_student_x(jax.random.fold_in(jax.random.fold_in(seeds[10], part), 71), part)
    student_z = normal_values(own_keys[1], (EXAMPLE_SPAN, LEARNER_COUNT * HEAD_DIM), 1.0, 6.0, ((0, 8),))
    student_b = normal_values(own_keys[2], (EXAMPLE_SPAN, GROUPS * STATE), STATE ** -0.5, 0.5, ((0, 8),))
    student_c = normal_values(own_keys[3], (EXAMPLE_SPAN, GROUPS * STATE), 1.0, 6.0, ((0, 8),))
    step_size = draw_step_size(jax.random.fold_in(jax.random.fold_in(seeds[10], part), 71), part)
    decay_rate = jnp.clip(jnp.exp(jax.random.uniform(seeds[5], (LEARNER_COUNT,), jnp.float32, math.log(0.5), math.log(2.0))), 0.5, 2.0)
    norm_gain = jnp.clip(1.0 + 0.1 * jax.random.normal(seeds[6], (LEARNER_COUNT * HEAD_DIM,), jnp.float32), 0.5, 1.5)
    teacher_q = draw_teacher_q(jax.random.fold_in(jax.random.fold_in(seeds[10], part), 71), part)
    teacher_k = draw_teacher_k(jax.random.fold_in(jax.random.fold_in(seeds[10], part), 71), part)
    teacher_v = normal_values(own_keys[9], (EXAMPLE_SPAN, KV_HEADS * HEAD_SIZE), 1.0, 6.0, ((0, 8),))
    return dict(student_x=student_x, student_z=student_z, student_b=student_b, student_c=student_c, step_size=step_size, decay_rate=decay_rate, norm_gain=norm_gain, teacher_q=teacher_q, teacher_k=teacher_k, teacher_v=teacher_v)


epsilon_norm = 1e-05
masked_score = -1e+30
HIGHEST = lax.Precision.HIGHEST

def block_pass(carry_state, block_inputs, decay_rate):
    x_block, b_block, c_block, step_block = block_inputs
    block_rows = x_block.shape[0]
    per_group = LEARNER_COUNT // GROUPS
    log_decay = -step_block * decay_rate[:, None]
    running = jnp.cumsum(log_decay, axis=1)
    b_three = b_block.reshape(block_rows, GROUPS, STATE).astype(jnp.float32)
    c_three = c_block.reshape(block_rows, GROUPS, STATE).astype(jnp.float32)
    x_four = x_block.reshape(block_rows, GROUPS, per_group, HEAD_DIM).astype(jnp.float32)
    products = jnp.einsum('tgn,sgn->gts', c_three, b_three, precision=HIGHEST)
    lower_mask = jnp.arange(block_rows)[:, None] >= jnp.arange(block_rows)[None, :]
    spread = running[:, :, None] - running[:, None, :]
    factor = jnp.exp(jnp.where(lower_mask[None], spread, masked_score))
    weights = (products[:, None] * factor.reshape(GROUPS, per_group, block_rows, block_rows)).astype(jnp.bfloat16)
    local_out = jnp.einsum('gkts,sgkp->tgkp', weights.astype(jnp.float32), x_four, precision=HIGHEST)
    state_four = carry_state.reshape(GROUPS, per_group, HEAD_DIM, STATE)
    carried = jnp.einsum('tgn,gkpn->tgkp', c_three, state_four, precision=HIGHEST)
    carried = carried * jnp.exp(running).T.reshape(block_rows, GROUPS, per_group, 1)
    tail_decay = jnp.exp(running[:, -1:] - running)
    scaled = x_four * tail_decay.T.reshape(block_rows, GROUPS, per_group, 1)
    fresh_state = jnp.einsum('sgkp,sgn->gkpn', scaled, b_three, precision=HIGHEST)
    new_state = jnp.exp(running[:, -1]).reshape(GROUPS, per_group, 1, 1) * state_four + fresh_state
    combined = (local_out + carried).reshape(block_rows, LEARNER_COUNT * HEAD_DIM)
    return (new_state.reshape(LEARNER_COUNT, HEAD_DIM, STATE), combined)

def student(student_x, student_z, student_b, student_c, step_size, decay_rate, norm_gain):
    block_count = EXAMPLE_SPAN // BLOCK
    blocks_in = (student_x.reshape(block_count, BLOCK, LEARNER_COUNT * HEAD_DIM), student_b.reshape(block_count, BLOCK, GROUPS * STATE), student_c.reshape(block_count, BLOCK, GROUPS * STATE), step_size.reshape(LEARNER_COUNT, block_count, BLOCK).transpose(1, 0, 2))

    def advance(carry_state, block_inputs):
        return block_pass(carry_state, block_inputs, decay_rate)
    zero_state = jnp.zeros((LEARNER_COUNT, HEAD_DIM, STATE), jnp.float32)
    _, block_outs = lax.scan(advance, zero_state, blocks_in)
    ssm_out = block_outs.reshape(EXAMPLE_SPAN, LEARNER_COUNT, HEAD_DIM)
    gated_out = ssm_out * jax.nn.silu(student_z.astype(jnp.float32)).reshape(EXAMPLE_SPAN, LEARNER_COUNT, HEAD_DIM)
    mean_square = lax.optimization_barrier(jnp.mean(gated_out * gated_out, axis=2, keepdims=True))
    normed = gated_out * lax.rsqrt(mean_square + epsilon_norm) * norm_gain.reshape(1, LEARNER_COUNT, HEAD_DIM)
    return normed.reshape(EXAMPLE_SPAN, LEARNER_COUNT * HEAD_DIM).astype(jnp.bfloat16)

def teacher(teacher_q, teacher_k, teacher_v):
    ratio = Q_HEADS // KV_HEADS
    query_rows = min(128, EXAMPLE_SPAN)
    block_count = EXAMPLE_SPAN // query_rows
    score_scale = 1.0 / HEAD_SIZE ** 0.5
    query_blocks = teacher_q.reshape(block_count, query_rows, KV_HEADS, ratio, HEAD_SIZE)
    keys_three = teacher_k.reshape(EXAMPLE_SPAN, KV_HEADS, HEAD_SIZE).astype(jnp.float32)
    values_three = teacher_v.reshape(EXAMPLE_SPAN, KV_HEADS, HEAD_SIZE).astype(jnp.float32)
    key_pos = jnp.arange(EXAMPLE_SPAN)

    def attend_rows(block_args):
        block_index, query_block = block_args
        scores = jnp.einsum('qgkd,sgd->qgks', query_block.astype(jnp.float32), keys_three, precision=HIGHEST) * score_scale
        query_pos = block_index * query_rows + jnp.arange(query_rows)
        visible = (key_pos[None, :] <= query_pos[:, None])[:, None, None, :]
        masked = jnp.where(visible, scores, masked_score)
        row_max = lax.optimization_barrier(jnp.max(masked, axis=3, keepdims=True))
        probabilities = jnp.where(visible, jnp.exp(masked - row_max), 0.0)
        row_total = lax.optimization_barrier(jnp.sum(probabilities, axis=3))
        low = probabilities.astype(jnp.bfloat16).astype(jnp.float32)
        weighted = jnp.einsum('qgks,sgd->qgkd', low, values_three, precision=HIGHEST)
        return (weighted / row_total[..., None]).astype(jnp.bfloat16)
    outputs = lax.map(attend_rows, (jnp.arange(block_count, dtype=jnp.int32), query_blocks))
    return outputs.reshape(EXAMPLE_SPAN, Q_HEADS * HEAD_SIZE)

def reference(student_x, student_z, student_b, student_c, step_size, decay_rate, norm_gain, teacher_q, teacher_k, teacher_v):
    student_out = student(student_x, student_z, student_b, student_c, step_size, decay_rate, norm_gain)
    teacher_out = teacher(teacher_q, teacher_k, teacher_v)
    return (student_out, teacher_out)
```

```python
import functools
import math

import jax
import jax.numpy as jnp
from jax import lax
from jax.experimental import pallas as pl
from jax.experimental.pallas import tpu as pltpu
from jax.sharding import PartitionSpec as P

GROUPS = 8
HEAD_SIZE = 128
BLOCK = 128

epsilon_norm = 1e-05
masked_score = -1e30
F32 = jnp.float32
BF16 = jnp.bfloat16
MESH = pl.DeviceIdType.MESH


def dot(a, b, ca=1, cb=0):
    return lax.dot_general(a, b, (((ca,), (cb,)), ((), ())), preferred_element_type=F32)


def kernel(
    n,
    x_hbm, z_hbm, b_hbm, c_hbm, step_hbm, rate_ref, gain_ref, q_hbm, k_hbm, v_hbm,
    sout_hbm, tout_hbm,
    x_ref, z_ref, b_ref, c_ref, step_ref, q_ref, kbuf, vbuf,
    cum_ref, ssm_ref, stl_ref, stin_ref, stout_ref,
    qt_ref, acc_ref, max_ref, sum_ref, so_ref, to_ref,
    in_sem, k_send, k_recv, v_send, v_recv, s_send, s_recv, so_sem, to_sem,
):
    me = lax.axis_index("seq")
    right = lax.rem(me + 1, n)
    left = lax.rem(me + n - 1, n)
    has_left = me > 0
    has_right = me < n - 1
    tokens, width = x_ref.shape
    heads = step_ref.shape[0]
    per_group = heads // GROUPS
    head_width = width // heads
    gw = width // GROUPS
    state_dim = b_ref.shape[1] // GROUPS
    kv_count = k_hbm.shape[1] // HEAD_SIZE
    qw = q_ref.shape[1] // kv_count
    ratio = qw // HEAD_SIZE
    lanes = 128
    pack = lanes // head_width
    scale = math.log2(math.e) / math.sqrt(HEAD_SIZE)

    loads = [
        pltpu.make_async_copy(src, dst, in_sem.at[i])
        for i, (src, dst) in enumerate(
            (
                (step_hbm, step_ref), (q_hbm, q_ref), (k_hbm, kbuf.at[me]), (v_hbm, vbuf.at[me]),
                (b_hbm, b_ref), (c_hbm, c_ref), (x_hbm, x_ref), (z_hbm, z_ref),
            )
        )
    ]
    for load in loads:
        load.start()

    barrier = pltpu.get_barrier_semaphore()

    @pl.when(has_left)
    def _():
        pl.semaphore_signal(barrier, inc=1, device_id={"seq": left}, device_id_type=MESH)

    @pl.when(has_right)
    def _():
        pl.semaphore_signal(barrier, inc=1, device_id={"seq": right}, device_id_type=MESH)

    pl.semaphore_wait(barrier, has_left.astype(jnp.int32) + has_right.astype(jnp.int32))

    def kv_copy(slot, k_src, v_src):
        return (
            pltpu.make_async_remote_copy(
                src_ref=k_src, dst_ref=kbuf.at[slot], send_sem=k_send.at[slot],
                recv_sem=k_recv.at[slot], device_id={"seq": right}, device_id_type=MESH,
            ),
            pltpu.make_async_remote_copy(
                src_ref=v_src, dst_ref=vbuf.at[slot], send_sem=v_send.at[slot],
                recv_sem=v_recv.at[slot], device_id={"seq": right}, device_id_type=MESH,
            ),
        )

    def state_copy(g):
        return pltpu.make_async_remote_copy(
            src_ref=stout_ref.at[g], dst_ref=stin_ref.at[g], send_sem=s_send.at[g],
            recv_sem=s_recv.at[g], device_id={"seq": right}, device_id_type=MESH,
        )

    @pl.when(has_right)
    def _():
        for copy in kv_copy(me, k_hbm, v_hbm):
            copy.start()

    def span(g, size):
        return pl.ds(pl.multiple_of(g * size, 128), size)

    loads[0].wait()
    eye = lax.broadcasted_iota(jnp.int32, (heads, heads), 0) == lax.broadcasted_iota(
        jnp.int32, (heads, heads), 1
    )
    rate = jnp.sum(jnp.where(eye, rate_ref[...], 0.0), axis=1, keepdims=True)
    running = -step_ref[...] * rate
    position = lax.broadcasted_iota(jnp.int32, (heads, tokens), 1)
    shift = 1
    while shift < tokens:
        running = running + jnp.where(position >= shift, pltpu.roll(running, shift, 1), 0.0)
        shift *= 2
    cum_ref[...] = running

    loads[1].wait()
    loads[2].wait()
    loads[3].wait()
    key_at = lax.broadcasted_iota(jnp.int32, (tokens, tokens), 0)
    query_at = lax.broadcasted_iota(jnp.int32, (tokens, tokens), 1)
    visible = jnp.concatenate([(key_at <= query_at).astype(F32)] * ratio, axis=1) > 0.5

    @pl.loop(0, kv_count)
    def _(g):
        for h in range(ratio):
            piece = q_ref[:, pl.ds(pl.multiple_of(g * qw + h * HEAD_SIZE, 128), HEAD_SIZE)]
            qt_ref[g, :, h * HEAD_SIZE : (h + 1) * HEAD_SIZE] = piece.T
        scores = dot(kbuf[me, :, span(g, HEAD_SIZE)], qt_ref[g]) * scale
        scores = jnp.where(visible, scores, masked_score)
        top = jnp.max(scores, axis=0, keepdims=True)
        weight = jnp.exp2(scores - top)
        max_ref[g] = top
        sum_ref[g] = jnp.sum(weight, axis=0, keepdims=True)
        acc_ref[g] = dot(vbuf[me, :, span(g, HEAD_SIZE)], weight.astype(BF16), 0, 0)

    for load in loads[4:]:
        load.wait()

    lower = query_at <= key_at
    low_half = lax.broadcasted_iota(jnp.int32, (tokens, lanes), 1) // head_width

    def spread(columns, p):
        out = columns[:, p * pack : p * pack + 1]
        for j in range(1, pack):
            at = p * pack + j
            out = jnp.where(low_half == j, columns[:, at : at + 1], out)
        return jnp.broadcast_to(out, (columns.shape[0], lanes))

    def student_local(g):
        cum = cum_ref[pl.ds(pl.multiple_of(g * per_group, 8), per_group), :]
        cum_t = cum.T
        tail_t = jnp.exp(cum[:, tokens - 1 : tokens] - cum).T
        b = b_ref[:, span(g, state_dim)]
        c = c_ref[:, span(g, state_dim)]
        products = dot(c, b, 1, 1)
        scaled = []
        for p in range(per_group // pack):
            x = x_ref[:, pl.ds(pl.multiple_of(g * gw + p * lanes, 128), lanes)].astype(F32)
            mixes = []
            sources = []
            for j in range(pack):
                h = p * pack + j
                difference = jnp.where(lower, cum_t[:, h : h + 1] - cum[h : h + 1, :], masked_score)
                mixes.append((products * jnp.exp(difference)).astype(BF16))
                sources.append(jnp.where(low_half == j, x, 0.0).astype(BF16))
            ssm_ref[g, :, p * lanes : (p + 1) * lanes] = dot(
                jnp.concatenate(mixes, axis=1), jnp.concatenate(sources, axis=0)
            )
            scaled.append((x * spread(tail_t, p)).astype(BF16))
        stl_ref[g] = dot(b, jnp.concatenate(scaled, axis=1), 0, 0)

    def attend(slot):
        @pl.loop(0, kv_count)
        def _(g):
            scores = dot(kbuf[slot, :, span(g, HEAD_SIZE)], qt_ref[g]) * scale
            old = max_ref[g]
            top = jnp.maximum(old, jnp.max(scores, axis=0, keepdims=True))
            shrink = jnp.exp2(old - top)
            weight = jnp.exp2(scores - top)
            max_ref[g] = top
            sum_ref[g] = sum_ref[g] * shrink + jnp.sum(weight, axis=0, keepdims=True)
            acc_ref[g] = acc_ref[g] * shrink + dot(
                vbuf[slot, :, span(g, HEAD_SIZE)], weight.astype(BF16), 0, 0
            )

    @pl.loop(0, max(n, GROUPS))
    def _(r):
        @pl.when(r < GROUPS)
        def _():
            student_local(r)

        @pl.when(r < me)
        def _():
            slot = me - 1 - r
            k_copy, v_copy = kv_copy(slot, kbuf.at[slot], vbuf.at[slot])
            k_copy.wait_recv()

            @pl.when(has_right)
            def _():
                k_copy.start()

            v_copy.wait_recv()

            @pl.when(has_right)
            def _():
                v_copy.start()

            attend(slot)

    @pl.loop(0, kv_count)
    def _(g):
        result = acc_ref[g] / sum_ref[g]
        for h in range(ratio):
            to_ref[:, pl.ds(pl.multiple_of(g * qw + h * HEAD_SIZE, 128), HEAD_SIZE)] = (
                result[:, h * HEAD_SIZE : (h + 1) * HEAD_SIZE].T.astype(BF16)
            )

    t_copy = pltpu.make_async_copy(to_ref, tout_hbm, to_sem)
    t_copy.start()

    @pl.when(me == 0)
    def _():
        stin_ref[...] = jnp.zeros_like(stin_ref)

    mean_of = jnp.where(
        lax.broadcasted_iota(jnp.int32, (lanes, lanes), 0) // head_width
        == lax.broadcasted_iota(jnp.int32, (lanes, lanes), 1) // head_width,
        1.0 / head_width,
        0.0,
    ).astype(BF16)
    row_half = lax.broadcasted_iota(jnp.int32, (1, lanes), 1) // head_width

    def out_copy(g):
        return pltpu.make_async_copy(
            so_ref.at[g], sout_hbm.at[:, span(g, gw)], so_sem.at[g]
        )

    @pl.loop(0, GROUPS)
    def _(g):
        cum = cum_ref[pl.ds(pl.multiple_of(g * per_group, 8), per_group), :]
        total = jnp.exp(cum[:, tokens - 1 : tokens])
        reach_t = jnp.exp(cum).T
        c = c_ref[:, span(g, state_dim)]

        @pl.when(has_left)
        def _():
            state_copy(g).wait_recv()

        state = stin_ref[g]

        @pl.when(has_right)
        def _():
            for p in range(per_group // pack):
                at = slice(p * lanes, (p + 1) * lanes)
                decay = total[p * pack : p * pack + 1, :]
                for j in range(1, pack):
                    decay = jnp.where(row_half == j, total[p * pack + j : p * pack + j + 1, :], decay)
                stout_ref[g, :, at] = (
                    state[:, at].astype(F32) * decay + stl_ref[g, :, at]
                ).astype(BF16)
            state_copy(g).start()

        carried = dot(c, state)
        for p in range(per_group // pack):
            at = slice(p * lanes, (p + 1) * lanes)
            cols = pl.ds(pl.multiple_of(g * gw + p * lanes, 128), lanes)
            ssm = ssm_ref[g, :, at] + carried[:, at] * spread(reach_t, p)
            z = z_ref[:, cols].astype(F32)
            gated = ssm * (z / (1.0 + jnp.exp(-z)))
            square = gated * gated
            high = square.astype(BF16)
            low = (square - high.astype(F32)).astype(BF16)
            mean = dot(high, mean_of) + dot(low, mean_of)
            so_ref[g, :, at] = (
                gated * lax.rsqrt(mean + epsilon_norm) * gain_ref[:, cols]
            ).astype(BF16)
        out_copy(g).start()

    t_copy.wait()

    @pl.loop(0, GROUPS)
    def _(g):
        out_copy(g).wait()

        @pl.when(has_right)
        def _():
            state_copy(g).wait_send()

    @pl.when(has_right)
    def _():
        for copy in kv_copy(me, k_hbm, v_hbm):
            copy.wait_send()

        @pl.loop(0, me)
        def _(slot):
            for copy in kv_copy(slot, kbuf.at[slot], vbuf.at[slot]):
                copy.wait_send()


def on_device(
    student_x, student_z, student_b, student_c, step_size, decay_rate, norm_gain,
    teacher_q, teacher_k, teacher_v,
):
    n = lax.axis_size("seq")
    tokens, width = student_x.shape
    heads = step_size.shape[0]
    assert tokens == BLOCK
    gw = width // GROUPS
    state_dim = student_b.shape[1] // GROUPS
    kv_count = teacher_k.shape[1] // HEAD_SIZE
    qw = teacher_q.shape[1] // kv_count
    hbm = pl.BlockSpec(memory_space=pl.ANY)
    vmem = pl.BlockSpec(memory_space=pltpu.VMEM)
    dma = pltpu.SemaphoreType.DMA
    return pl.pallas_call(
        functools.partial(kernel, n),
        out_shape=(
            jax.ShapeDtypeStruct(student_x.shape, BF16),
            jax.ShapeDtypeStruct(teacher_q.shape, BF16),
        ),
        in_specs=[hbm, hbm, hbm, hbm, hbm, vmem, vmem, hbm, hbm, hbm],
        out_specs=(hbm, hbm),
        scratch_shapes=[
            pltpu.VMEM(student_x.shape, BF16),
            pltpu.VMEM(student_z.shape, BF16),
            pltpu.VMEM(student_b.shape, BF16),
            pltpu.VMEM(student_c.shape, BF16),
            pltpu.VMEM(step_size.shape, F32),
            pltpu.VMEM(teacher_q.shape, BF16),
            pltpu.VMEM((n,) + teacher_k.shape, BF16),
            pltpu.VMEM((n,) + teacher_v.shape, BF16),
            pltpu.VMEM(step_size.shape, F32),
            pltpu.VMEM((GROUPS, tokens, gw), F32),
            pltpu.VMEM((GROUPS, state_dim, gw), F32),
            pltpu.VMEM((GROUPS, state_dim, gw), BF16),
            pltpu.VMEM((GROUPS, state_dim, gw), BF16),
            pltpu.VMEM((kv_count, HEAD_SIZE, qw), BF16),
            pltpu.VMEM((kv_count, HEAD_SIZE, qw), F32),
            pltpu.VMEM((kv_count, 1, qw), F32),
            pltpu.VMEM((kv_count, 1, qw), F32),
            pltpu.VMEM((GROUPS, tokens, gw), BF16),
            pltpu.VMEM(teacher_q.shape, BF16),
            dma((8,)),
            dma((n,)),
            dma((n,)),
            dma((n,)),
            dma((n,)),
            dma((GROUPS,)),
            dma((GROUPS,)),
            dma((GROUPS,)),
            dma,
        ],
        compiler_params=pltpu.CompilerParams(
            collective_id=0, has_side_effects=True, vmem_limit_bytes=56 * 1024 * 1024
        ),
    )(
        student_x, student_z, student_b, student_c, step_size, decay_rate[None, :],
        norm_gain[None, :], teacher_q, teacher_k, teacher_v,
    )


def solution(mesh):
    return jax.shard_map(
        on_device,
        mesh=mesh,
        in_specs=(
            P(("dp", "seq"), None),
            P(("dp", "seq"), None),
            P(("dp", "seq"), None),
            P(("dp", "seq"), None),
            P(None, ("dp", "seq")),
            P(),
            P(),
            P(("dp", "seq"), None),
            P(("dp", "seq"), None),
            P(("dp", "seq"), None),
        ),
        out_specs=(P(("dp", "seq"), None), P(("dp", "seq"), None)),
        check_vma=False,
    )
```

```python
import functools
import math

import jax
import jax.numpy as jnp
from jax import lax
from jax.experimental import pallas as pl
from jax.experimental.pallas import tpu as pltpu
from jax.sharding import PartitionSpec as P

GROUPS = 8
HEAD_SIZE = 128
BLOCK = 128
CUTS = 2

epsilon_norm = 1e-05
masked_score = -1e30
F32 = jnp.float32
BF16 = jnp.bfloat16
MESH = pl.DeviceIdType.MESH


def dot(a, b, ca=1, cb=0):
    return lax.dot_general(a, b, (((ca,), (cb,)), ((), ())), preferred_element_type=F32)


def kernel(
    n,
    x_hbm, z_hbm, b_hbm, c_hbm, step_hbm, rate_ref, gain_ref, q_hbm, k_hbm, v_hbm,
    so_ref, to_ref,
    x_ref, z_ref, b_ref, c_ref, step_ref, q_ref, kbuf, vbuf,
    cum_ref, ssm_ref, reach_ref, stl_ref, stin_ref, stout_ref,
    qt_ref, acc_ref, max_ref, sum_ref,
    in_sem, k_send, k_recv, v_send, v_recv, s_send, s_recv,
):
    me = lax.axis_index("seq")
    right = lax.rem(me + 1, n)
    left = lax.rem(me + n - 1, n)
    has_left = me > 0
    has_right = me < n - 1
    tokens, width = x_ref.shape
    heads = step_ref.shape[0]
    per_group = heads // GROUPS
    head_width = width // heads
    gw = width // GROUPS
    state_dim = b_ref.shape[1] // GROUPS
    kv_count = k_hbm.shape[1] // HEAD_SIZE
    qw = q_ref.shape[1] // kv_count
    ratio = qw // HEAD_SIZE
    lanes = 128
    pack = lanes // head_width
    scale = math.log2(math.e) / math.sqrt(HEAD_SIZE)

    loads = [
        pltpu.make_async_copy(src, dst, in_sem.at[i])
        for i, (src, dst) in enumerate(
            (
                (step_hbm, step_ref), (q_hbm, q_ref), (k_hbm, kbuf.at[me]), (v_hbm, vbuf.at[me]),
                (b_hbm, b_ref), (c_hbm, c_ref), (x_hbm, x_ref), (z_hbm, z_ref),
            )
        )
    ]
    for load in loads:
        load.start()

    barrier = pltpu.get_barrier_semaphore()

    @pl.when(has_left)
    def _():
        pl.semaphore_signal(barrier, inc=1, device_id={"seq": left}, device_id_type=MESH)

    @pl.when(has_right)
    def _():
        pl.semaphore_signal(barrier, inc=1, device_id={"seq": right}, device_id_type=MESH)

    pl.semaphore_wait(barrier, has_left.astype(jnp.int32) + has_right.astype(jnp.int32))

    def kv_copy(slot, k_src, v_src):
        return (
            pltpu.make_async_remote_copy(
                src_ref=k_src, dst_ref=kbuf.at[slot], send_sem=k_send.at[slot],
                recv_sem=k_recv.at[slot], device_id={"seq": right}, device_id_type=MESH,
            ),
            pltpu.make_async_remote_copy(
                src_ref=v_src, dst_ref=vbuf.at[slot], send_sem=v_send.at[slot],
                recv_sem=v_recv.at[slot], device_id={"seq": right}, device_id_type=MESH,
            ),
        )

    def state_copy(g, cut):
        return pltpu.make_async_remote_copy(
            src_ref=stout_ref.at[g, cut], dst_ref=stin_ref.at[g, cut], send_sem=s_send.at[g, cut],
            recv_sem=s_recv.at[g, cut], device_id={"seq": right}, device_id_type=MESH,
        )

    @pl.when(has_right)
    def _():
        for copy in kv_copy(me, k_hbm, v_hbm):
            copy.start()

    def span(g, size):
        return pl.ds(pl.multiple_of(g * size, 128), size)

    loads[0].wait()
    eye = lax.broadcasted_iota(jnp.int32, (heads, heads), 0) == lax.broadcasted_iota(
        jnp.int32, (heads, heads), 1
    )
    rate = jnp.sum(jnp.where(eye, rate_ref[...], 0.0), axis=1, keepdims=True)
    running = -step_ref[...] * rate
    position = lax.broadcasted_iota(jnp.int32, (heads, tokens), 1)
    shift = 1
    while shift < tokens:
        running = running + jnp.where(position >= shift, pltpu.roll(running, shift, 1), 0.0)
        shift *= 2
    cum_ref[...] = running

    key_at = lax.broadcasted_iota(jnp.int32, (tokens, tokens), 0)
    query_at = lax.broadcasted_iota(jnp.int32, (tokens, tokens), 1)
    half = lax.broadcasted_iota(jnp.int32, (tokens, lanes), 1) // head_width
    row_half = lax.broadcasted_iota(jnp.int32, (1, lanes), 1) // head_width
    pairs = per_group // pack
    cut_pairs = pairs // CUTS

    def spread(columns, p):
        out = columns[:, p * pack : p * pack + 1]
        for j in range(1, pack):
            at = p * pack + j
            out = jnp.where(half == j, columns[:, at : at + 1], out)
        return jnp.broadcast_to(out, (columns.shape[0], lanes))

    def columns_of(g, p):
        return pl.ds(pl.multiple_of(g * gw + p * lanes, 128), lanes)

    loads[4].wait()
    loads[6].wait()

    @pl.loop(0, GROUPS)
    def _(g):
        cum = cum_ref[pl.ds(pl.multiple_of(g * per_group, 8), per_group), :]
        tail_t = jnp.exp(cum[:, tokens - 1 : tokens] - cum).T
        scaled = [
            (x_ref[:, columns_of(g, p)].astype(F32) * spread(tail_t, p)).astype(BF16)
            for p in range(pairs)
        ]
        added = dot(b_ref[:, span(g, state_dim)], jnp.concatenate(scaled, axis=1), 0, 0)
        stl_ref[g] = added

        @pl.when(me == 0)
        def _():
            for cut in range(CUTS):
                size = gw // CUTS
                stout_ref[g, cut] = added[:, cut * size : (cut + 1) * size].astype(BF16)
                stin_ref[g, cut] = jnp.zeros((state_dim, size), BF16)

    @pl.when(jnp.logical_and(me == 0, has_right))
    def _():
        @pl.loop(0, GROUPS)
        def _(g):
            for cut in range(CUTS):
                state_copy(g, cut).start()

    def relay(slot):
        k_copy, v_copy = kv_copy(slot, kbuf.at[slot], vbuf.at[slot])
        k_copy.wait_recv()

        @pl.when(has_right)
        def _():
            k_copy.start()

        v_copy.wait_recv()

        @pl.when(has_right)
        def _():
            v_copy.start()

    near = lax.rem(me, 2) == 1

    @pl.when(near)
    def _():
        relay(me - 1)

    for i in (1, 2, 3):
        loads[i].wait()
    visible = jnp.concatenate([(key_at <= query_at).astype(F32)] * ratio, axis=1) > 0.5

    @pl.loop(0, kv_count)
    def _(g):
        for h in range(ratio):
            piece = q_ref[:, pl.ds(pl.multiple_of(g * qw + h * HEAD_SIZE, 128), HEAD_SIZE)]
            qt_ref[g, :, h * HEAD_SIZE : (h + 1) * HEAD_SIZE] = piece.T
        scores = dot(kbuf[me, :, span(g, HEAD_SIZE)], qt_ref[g]) * scale
        scores = jnp.where(visible, scores, masked_score)
        top = jnp.max(scores, axis=0, keepdims=True)
        weight = jnp.exp2(scores - top)
        max_ref[g] = top
        sum_ref[g] = jnp.sum(weight, axis=0, keepdims=True)
        acc_ref[g] = dot(vbuf[me, :, span(g, HEAD_SIZE)], weight.astype(BF16), 0, 0)

    loads[5].wait()
    loads[7].wait()
    lower = query_at <= key_at

    def student_local(g):
        cum = cum_ref[pl.ds(pl.multiple_of(g * per_group, 8), per_group), :]
        cum_t = cum.T
        reach_t = jnp.exp(cum).T
        products = dot(c_ref[:, span(g, state_dim)], b_ref[:, span(g, state_dim)], 1, 1)
        for p in range(pairs):
            x = x_ref[:, columns_of(g, p)].astype(F32)
            mixes = []
            sources = []
            for j in range(pack):
                h = p * pack + j
                difference = jnp.where(lower, cum_t[:, h : h + 1] - cum[h : h + 1, :], masked_score)
                mixes.append((products * jnp.exp(difference)).astype(BF16))
                sources.append(jnp.where(half == j, x, 0.0).astype(BF16))
            z = z_ref[:, columns_of(g, p)].astype(F32)
            gate = z / (1.0 + jnp.exp(-z))
            at = slice(p * lanes, (p + 1) * lanes)
            ssm_ref[g, :, at] = gate * dot(
                jnp.concatenate(mixes, axis=1), jnp.concatenate(sources, axis=0)
            )
            reach_ref[g, :, at] = gate * spread(reach_t, p)

    def attend(slot):
        @pl.loop(0, kv_count)
        def _(g):
            scores = dot(kbuf[slot, :, span(g, HEAD_SIZE)], qt_ref[g]) * scale
            old = max_ref[g]
            top = jnp.maximum(old, jnp.max(scores, axis=0, keepdims=True))
            shrink = jnp.exp2(old - top)
            weight = jnp.exp2(scores - top)
            max_ref[g] = top
            sum_ref[g] = sum_ref[g] * shrink + jnp.sum(weight, axis=0, keepdims=True)
            acc_ref[g] = acc_ref[g] * shrink + dot(
                vbuf[slot, :, span(g, HEAD_SIZE)], weight.astype(BF16), 0, 0
            )

    @pl.loop(0, max(n, GROUPS))
    def _(r):
        @pl.when(r < GROUPS)
        def _():
            student_local(r)

        @pl.when(r < me)
        def _():
            @pl.when(jnp.logical_or(r > 0, jnp.logical_not(near)))
            def _():
                relay(me - 1 - r)

            attend(me - 1 - r)

    @pl.loop(0, kv_count)
    def _(g):
        result = acc_ref[g] / sum_ref[g]
        for h in range(ratio):
            to_ref[:, pl.ds(pl.multiple_of(g * qw + h * HEAD_SIZE, 128), HEAD_SIZE)] = (
                result[:, h * HEAD_SIZE : (h + 1) * HEAD_SIZE].T.astype(BF16)
            )

    mean_of = jnp.where(
        lax.broadcasted_iota(jnp.int32, (lanes, lanes), 0) // head_width
        == lax.broadcasted_iota(jnp.int32, (lanes, lanes), 1) // head_width,
        1.0 / head_width,
        0.0,
    ).astype(BF16)

    @pl.loop(0, GROUPS)
    def _(g):
        cum = cum_ref[pl.ds(pl.multiple_of(g * per_group, 8), per_group), :]
        total = jnp.exp(cum[:, tokens - 1 : tokens])
        c = c_ref[:, span(g, state_dim)]
        for cut in range(CUTS):

            @pl.when(has_left)
            def _():
                state_copy(g, cut).wait_recv()

            state = stin_ref[g, cut]

            @pl.when(jnp.logical_and(has_left, has_right))
            def _():
                for i in range(cut_pairs):
                    p = cut * cut_pairs + i
                    at = slice(i * lanes, (i + 1) * lanes)
                    decay = total[p * pack : p * pack + 1, :]
                    for j in range(1, pack):
                        decay = jnp.where(
                            row_half == j, total[p * pack + j : p * pack + j + 1, :], decay
                        )
                    stout_ref[g, cut, :, at] = (
                        state[:, at].astype(F32) * decay
                        + stl_ref[g, :, p * lanes : (p + 1) * lanes]
                    ).astype(BF16)
                state_copy(g, cut).start()

            carried = dot(c, state)
            for i in range(cut_pairs):
                p = cut * cut_pairs + i
                at = slice(p * lanes, (p + 1) * lanes)
                gated = ssm_ref[g, :, at] + reach_ref[g, :, at] * carried[:, i * lanes : (i + 1) * lanes]
                mean = dot((gated * gated).astype(BF16), mean_of)
                so_ref[:, columns_of(g, p)] = (
                    gated * lax.rsqrt(mean + epsilon_norm) * gain_ref[:, columns_of(g, p)]
                ).astype(BF16)

    @pl.when(has_right)
    def _():
        @pl.loop(0, GROUPS)
        def _(g):
            for cut in range(CUTS):
                state_copy(g, cut).wait_send()

        for copy in kv_copy(me, k_hbm, v_hbm):
            copy.wait_send()

        @pl.loop(0, me)
        def _(slot):
            for copy in kv_copy(slot, kbuf.at[slot], vbuf.at[slot]):
                copy.wait_send()


def store(s_ref, t_ref, s_out, t_out, sem):
    copies = [
        pltpu.make_async_copy(s_ref, s_out, sem.at[0]),
        pltpu.make_async_copy(t_ref, t_out, sem.at[1]),
    ]
    for copy in copies:
        copy.start()
    for copy in copies:
        copy.wait()


def on_device(
    student_x, student_z, student_b, student_c, step_size, decay_rate, norm_gain,
    teacher_q, teacher_k, teacher_v,
):
    n = lax.axis_size("seq")
    tokens, width = student_x.shape
    heads = step_size.shape[0]
    assert tokens == BLOCK
    gw = width // GROUPS
    state_dim = student_b.shape[1] // GROUPS
    kv_count = teacher_k.shape[1] // HEAD_SIZE
    qw = teacher_q.shape[1] // kv_count
    hbm = pl.BlockSpec(memory_space=pl.ANY)
    vmem = pl.BlockSpec(memory_space=pltpu.VMEM)
    dma = pltpu.SemaphoreType.DMA
    results = pl.pallas_call(
        functools.partial(kernel, n),
        out_shape=(
            pltpu.VMEM(student_x.shape, BF16),
            pltpu.VMEM(teacher_q.shape, BF16),
        ),
        in_specs=[hbm, hbm, hbm, hbm, hbm, vmem, vmem, hbm, hbm, hbm],
        out_specs=(vmem, vmem),
        scratch_shapes=[
            pltpu.VMEM(student_x.shape, BF16),
            pltpu.VMEM(student_z.shape, BF16),
            pltpu.VMEM(student_b.shape, BF16),
            pltpu.VMEM(student_c.shape, BF16),
            pltpu.VMEM(step_size.shape, F32),
            pltpu.VMEM(teacher_q.shape, BF16),
            pltpu.VMEM((n,) + teacher_k.shape, BF16),
            pltpu.VMEM((n,) + teacher_v.shape, BF16),
            pltpu.VMEM(step_size.shape, F32),
            pltpu.VMEM((GROUPS, tokens, gw), F32),
            pltpu.VMEM((GROUPS, tokens, gw), F32),
            pltpu.VMEM((GROUPS, state_dim, gw), F32),
            pltpu.VMEM((GROUPS, CUTS, state_dim, gw // CUTS), BF16),
            pltpu.VMEM((GROUPS, CUTS, state_dim, gw // CUTS), BF16),
            pltpu.VMEM((kv_count, HEAD_SIZE, qw), BF16),
            pltpu.VMEM((kv_count, HEAD_SIZE, qw), F32),
            pltpu.VMEM((kv_count, 1, qw), F32),
            pltpu.VMEM((kv_count, 1, qw), F32),
            dma((8,)),
            dma((n,)),
            dma((n,)),
            dma((n,)),
            dma((n,)),
            dma((GROUPS, CUTS)),
            dma((GROUPS, CUTS)),
        ],
        compiler_params=pltpu.CompilerParams(
            collective_id=0, has_side_effects=True, vmem_limit_bytes=56 * 1024 * 1024
        ),
    )(
        student_x, student_z, student_b, student_c, step_size, decay_rate[None, :],
        norm_gain[None, :], teacher_q, teacher_k, teacher_v,
    )
    results = [pltpu.with_memory_space_constraint(r, pltpu.VMEM) for r in results]
    return pl.pallas_call(
        store,
        out_shape=(
            jax.ShapeDtypeStruct(student_x.shape, BF16),
            jax.ShapeDtypeStruct(teacher_q.shape, BF16),
        ),
        in_specs=[vmem, vmem],
        out_specs=(hbm, hbm),
        scratch_shapes=[dma((2,))],
    )(*results)


def solution(mesh):
    return jax.shard_map(
        on_device,
        mesh=mesh,
        in_specs=(
            P(("dp", "seq"), None),
            P(("dp", "seq"), None),
            P(("dp", "seq"), None),
            P(("dp", "seq"), None),
            P(None, ("dp", "seq")),
            P(),
            P(),
            P(("dp", "seq"), None),
            P(("dp", "seq"), None),
            P(("dp", "seq"), None),
        ),
        out_specs=(P(("dp", "seq"), None), P(("dp", "seq"), None)),
        check_vma=False,
    )
```

```python
import functools
import math

import jax
import jax.numpy as jnp
from jax import lax
from jax.experimental import pallas as pl
from jax.experimental.pallas import tpu as pltpu
from jax.sharding import PartitionSpec as P

GROUPS = 8
HEAD_SIZE = 128
BLOCK = 128
CUTS = 2

epsilon_norm = 1e-05
masked_score = -1e30
F32 = jnp.float32
BF16 = jnp.bfloat16
MESH = pl.DeviceIdType.MESH


def dot(a, b, ca=1, cb=0):
    return lax.dot_general(a, b, (((ca,), (cb,)), ((), ())), preferred_element_type=F32)


def kernel(
    n,
    x_hbm, z_hbm, b_hbm, c_hbm, step_hbm, rate_ref, gain_ref, q_hbm, k_hbm, v_hbm,
    so_ref, to_ref,
    x_ref, z_ref, b_ref, c_ref, step_ref, q_ref, kbuf, vbuf,
    cum_ref, ssm_ref, reach_ref, stl_ref, stin_ref, stout_ref,
    qt_ref, acc_ref, max_ref, sum_ref,
    in_sem, k_send, k_recv, v_send, v_recv, s_send, s_recv,
):
    me = lax.axis_index("seq")
    right = lax.rem(me + 1, n)
    left = lax.rem(me + n - 1, n)
    has_left = me > 0
    has_right = me < n - 1
    tokens, width = x_ref.shape
    heads = step_ref.shape[0]
    per_group = heads // GROUPS
    head_width = width // heads
    gw = width // GROUPS
    state_dim = b_ref.shape[1] // GROUPS
    kv_count = k_hbm.shape[1] // HEAD_SIZE
    qw = q_ref.shape[1] // kv_count
    ratio = qw // HEAD_SIZE
    lanes = 128
    pack = lanes // head_width
    scale = math.log2(math.e) / math.sqrt(HEAD_SIZE)

    loads = [
        pltpu.make_async_copy(src, dst, in_sem.at[i])
        for i, (src, dst) in enumerate(
            (
                (step_hbm, step_ref), (q_hbm, q_ref), (k_hbm, kbuf.at[me]), (v_hbm, vbuf.at[me]),
                (b_hbm, b_ref), (c_hbm, c_ref), (x_hbm, x_ref), (z_hbm, z_ref),
            )
        )
    ]
    for load in loads:
        load.start()

    barrier = pltpu.get_barrier_semaphore()

    @pl.when(has_left)
    def _():
        pl.semaphore_signal(barrier, inc=1, device_id={"seq": left}, device_id_type=MESH)

    @pl.when(has_right)
    def _():
        pl.semaphore_signal(barrier, inc=1, device_id={"seq": right}, device_id_type=MESH)

    pl.semaphore_wait(barrier, has_left.astype(jnp.int32) + has_right.astype(jnp.int32))

    def key_copy(slot, source):
        return pltpu.make_async_remote_copy(
            src_ref=source, dst_ref=kbuf.at[slot], send_sem=k_send.at[slot],
            recv_sem=k_recv.at[slot], device_id={"seq": right}, device_id_type=MESH,
        )

    def value_copy(slot, source):
        return pltpu.make_async_remote_copy(
            src_ref=source, dst_ref=vbuf.at[slot], send_sem=v_send.at[slot],
            recv_sem=v_recv.at[slot], device_id={"seq": right}, device_id_type=MESH,
        )

    def state_copy(g, cut):
        return pltpu.make_async_remote_copy(
            src_ref=stout_ref.at[g, cut], dst_ref=stin_ref.at[g, cut], send_sem=s_send.at[g, cut],
            recv_sem=s_recv.at[g, cut], device_id={"seq": right}, device_id_type=MESH,
        )

    @pl.when(has_right)
    def _():
        for copy in (key_copy(me, k_hbm), value_copy(me, v_hbm)):
            copy.start()

    def span(g, size):
        return pl.ds(pl.multiple_of(g * size, 128), size)

    loads[0].wait()
    eye = lax.broadcasted_iota(jnp.int32, (heads, heads), 0) == lax.broadcasted_iota(
        jnp.int32, (heads, heads), 1
    )
    rate = jnp.sum(jnp.where(eye, rate_ref[...], 0.0), axis=1, keepdims=True)
    running = -step_ref[...] * rate
    position = lax.broadcasted_iota(jnp.int32, (heads, tokens), 1)
    shift = 1
    while shift < tokens:
        running = running + jnp.where(position >= shift, pltpu.roll(running, shift, 1), 0.0)
        shift *= 2
    cum_ref[...] = running

    key_at = lax.broadcasted_iota(jnp.int32, (tokens, tokens), 0)
    query_at = lax.broadcasted_iota(jnp.int32, (tokens, tokens), 1)
    half = lax.broadcasted_iota(jnp.int32, (tokens, lanes), 1) // head_width
    row_half = lax.broadcasted_iota(jnp.int32, (1, lanes), 1) // head_width
    pairs = per_group // pack
    cut_pairs = pairs // CUTS

    def columns_of(g, p):
        return pl.ds(pl.multiple_of(g * gw + p * lanes, 128), lanes)

    def relay_key(slot):
        copy = key_copy(slot, kbuf.at[slot])
        copy.wait_recv()

        @pl.when(has_right)
        def _():
            copy.start()

    def relay_value(slot):
        copy = value_copy(slot, vbuf.at[slot])
        copy.wait_recv()

        @pl.when(has_right)
        def _():
            copy.start()

    visible = jnp.concatenate([(key_at <= query_at).astype(F32)] * ratio, axis=1) > 0.5

    def attend_own(g):
        for h in range(ratio):
            piece = q_ref[:, pl.ds(pl.multiple_of(g * qw + h * HEAD_SIZE, 128), HEAD_SIZE)]
            qt_ref[g, :, h * HEAD_SIZE : (h + 1) * HEAD_SIZE] = piece.T
        scores = dot(kbuf[me, :, span(g, HEAD_SIZE)], qt_ref[g]) * scale
        scores = jnp.where(visible, scores, masked_score)
        top = jnp.max(scores, axis=0, keepdims=True)
        weight = jnp.exp2(scores - top)
        max_ref[g] = top
        sum_ref[g] = jnp.sum(weight, axis=0, keepdims=True)
        acc_ref[g] = dot(vbuf[me, :, span(g, HEAD_SIZE)], weight.astype(BF16), 0, 0)

    for load in loads[1:]:
        load.wait()
    lower = query_at <= key_at

    def student_local(g):
        cum = cum_ref[pl.ds(pl.multiple_of(g * per_group, 8), per_group), :]
        cum_t = cum.T
        tail = jnp.exp(cum[:, tokens - 1 : tokens] - cum)
        b = b_ref[:, span(g, state_dim)]
        b_t = b.T.astype(F32)
        products = dot(c_ref[:, span(g, state_dim)], b, 1, 1)
        for p in range(pairs):
            x = x_ref[:, columns_of(g, p)].astype(F32)
            mixes = []
            adds = []
            sources = []
            reach = None
            for j in range(pack):
                h = p * pack + j
                column = jnp.broadcast_to(cum_t[:, h : h + 1], (tokens, lanes))
                difference = jnp.where(lower, column - cum[h : h + 1, :], masked_score)
                mixes.append((products * jnp.exp(difference)).astype(BF16))
                adds.append((b_t * tail[h : h + 1, :]).astype(BF16))
                sources.append(jnp.where(half == j, x, 0.0).astype(BF16))
                reach = column if j == 0 else jnp.where(half == j, column, reach)
            z = z_ref[:, columns_of(g, p)].astype(F32)
            gate = z / (1.0 + jnp.exp(-z))
            at = slice(p * lanes, (p + 1) * lanes)
            source = jnp.concatenate(sources, axis=0)
            ssm_ref[g, :, at] = gate * dot(jnp.concatenate(mixes, axis=1), source)
            reach_ref[g, :, at] = gate * jnp.exp(reach)
            stl_ref[g, :, at] = dot(jnp.concatenate(adds, axis=1), source)

        @pl.when(me == 0)
        def _():
            for cut in range(CUTS):
                size = gw // CUTS
                stout_ref[g, cut] = stl_ref[g, :, cut * size : (cut + 1) * size].astype(BF16)
                stin_ref[g, cut] = jnp.zeros((state_dim, size), BF16)

    def attend(slot):
        @pl.loop(0, kv_count)
        def _(g):
            scores = dot(kbuf[slot, :, span(g, HEAD_SIZE)], qt_ref[g]) * scale
            old = max_ref[g]
            top = jnp.maximum(old, jnp.max(scores, axis=0, keepdims=True))
            shrink = jnp.exp2(old - top)
            weight = jnp.exp2(scores - top)
            max_ref[g] = top
            sum_ref[g] = sum_ref[g] * shrink + jnp.sum(weight, axis=0, keepdims=True)
            acc_ref[g] = acc_ref[g] * shrink + dot(
                vbuf[slot, :, span(g, HEAD_SIZE)], weight.astype(BF16), 0, 0
            )

    near = lax.rem(me, 2) == 1
    far = jnp.logical_not(near)
    pieces = 2 * me

    @pl.loop(0, GROUPS)
    def _(r):
        student_local(r)
        attend_own(r)
        piece = jnp.where(near, (r + 1) // 2, (r - 2) // 2)

        @pl.when(jnp.logical_and(near, r == 0))
        def _():
            relay_key(me - 1)
            relay_value(me - 1)

        turn = jnp.where(near, r - 3, r - 2)
        due = jnp.logical_and(turn >= 0, piece < pieces)

        @pl.when(jnp.logical_and(due, lax.rem(turn + 4, 4) == 0))
        def _():
            relay_key(me - 1 - piece // 2)

        @pl.when(jnp.logical_and(due, lax.rem(turn + 4, 4) == 2))
        def _():
            relay_value(me - 1 - piece // 2)

    @pl.when(jnp.logical_and(me == 0, has_right))
    def _():
        @pl.loop(0, GROUPS)
        def _(g):
            for cut in range(CUTS):
                state_copy(g, cut).start()

    first = jnp.where(near, GROUPS // 2 + 1, GROUPS // 2 - 1)

    @pl.loop(0, me)
    def _(j):
        attend(me - 1 - j)
        piece = first + 2 * j

        @pl.when(piece < pieces)
        def _():
            relay_value(me - 1 - piece // 2)

        @pl.when(piece + 1 < pieces)
        def _():
            relay_key(me - 1 - (piece + 1) // 2)

    @pl.loop(0, kv_count)
    def _(g):
        result = acc_ref[g] / sum_ref[g]
        for h in range(ratio):
            to_ref[:, pl.ds(pl.multiple_of(g * qw + h * HEAD_SIZE, 128), HEAD_SIZE)] = (
                result[:, h * HEAD_SIZE : (h + 1) * HEAD_SIZE].T.astype(BF16)
            )

    mean_of = jnp.where(
        lax.broadcasted_iota(jnp.int32, (lanes, lanes), 0) // head_width
        == lax.broadcasted_iota(jnp.int32, (lanes, lanes), 1) // head_width,
        1.0 / head_width,
        0.0,
    ).astype(BF16)

    @pl.loop(0, GROUPS)
    def _(g):
        cum = cum_ref[pl.ds(pl.multiple_of(g * per_group, 8), per_group), :]
        total = jnp.exp(cum[:, tokens - 1 : tokens])
        c = c_ref[:, span(g, state_dim)]
        for cut in range(CUTS):

            @pl.when(has_left)
            def _():
                state_copy(g, cut).wait_recv()

            state = stin_ref[g, cut]

            @pl.when(jnp.logical_and(has_left, has_right))
            def _():
                for i in range(cut_pairs):
                    p = cut * cut_pairs + i
                    at = slice(i * lanes, (i + 1) * lanes)
                    decay = total[p * pack : p * pack + 1, :]
                    for j in range(1, pack):
                        decay = jnp.where(
                            row_half == j, total[p * pack + j : p * pack + j + 1, :], decay
                        )
                    stout_ref[g, cut, :, at] = (
                        state[:, at].astype(F32) * decay
                        + stl_ref[g, :, p * lanes : (p + 1) * lanes]
                    ).astype(BF16)
                state_copy(g, cut).start()

            carried = dot(c, state)
            for i in range(cut_pairs):
                p = cut * cut_pairs + i
                at = slice(p * lanes, (p + 1) * lanes)
                gated = ssm_ref[g, :, at] + reach_ref[g, :, at] * carried[:, i * lanes : (i + 1) * lanes]
                mean = dot((gated * gated).astype(BF16), mean_of)
                so_ref[:, columns_of(g, p)] = (
                    gated * lax.rsqrt(mean + epsilon_norm) * gain_ref[:, columns_of(g, p)]
                ).astype(BF16)

    @pl.when(has_right)
    def _():
        @pl.loop(0, GROUPS)
        def _(g):
            for cut in range(CUTS):
                state_copy(g, cut).wait_send()

        for copy in (key_copy(me, k_hbm), value_copy(me, v_hbm)):
            copy.wait_send()

        @pl.loop(0, me)
        def _(slot):
            for copy in (key_copy(slot, kbuf.at[slot]), value_copy(slot, vbuf.at[slot])):
                copy.wait_send()


def store(s_ref, t_ref, s_out, t_out, sem):
    copies = [
        pltpu.make_async_copy(s_ref, s_out, sem.at[0]),
        pltpu.make_async_copy(t_ref, t_out, sem.at[1]),
    ]
    for copy in copies:
        copy.start()
    for copy in copies:
        copy.wait()


def on_device(
    student_x, student_z, student_b, student_c, step_size, decay_rate, norm_gain,
    teacher_q, teacher_k, teacher_v,
):
    n = lax.axis_size("seq")
    tokens, width = student_x.shape
    heads = step_size.shape[0]
    assert tokens == BLOCK
    gw = width // GROUPS
    state_dim = student_b.shape[1] // GROUPS
    kv_count = teacher_k.shape[1] // HEAD_SIZE
    qw = teacher_q.shape[1] // kv_count
    hbm = pl.BlockSpec(memory_space=pl.ANY)
    vmem = pl.BlockSpec(memory_space=pltpu.VMEM)
    dma = pltpu.SemaphoreType.DMA
    results = pl.pallas_call(
        functools.partial(kernel, n),
        out_shape=(
            pltpu.VMEM(student_x.shape, BF16),
            pltpu.VMEM(teacher_q.shape, BF16),
        ),
        in_specs=[hbm, hbm, hbm, hbm, hbm, vmem, vmem, hbm, hbm, hbm],
        out_specs=(vmem, vmem),
        scratch_shapes=[
            pltpu.VMEM(student_x.shape, BF16),
            pltpu.VMEM(student_z.shape, BF16),
            pltpu.VMEM(student_b.shape, BF16),
            pltpu.VMEM(student_c.shape, BF16),
            pltpu.VMEM(step_size.shape, F32),
            pltpu.VMEM(teacher_q.shape, BF16),
            pltpu.VMEM((n,) + teacher_k.shape, BF16),
            pltpu.VMEM((n,) + teacher_v.shape, BF16),
            pltpu.VMEM(step_size.shape, F32),
            pltpu.VMEM((GROUPS, tokens, gw), F32),
            pltpu.VMEM((GROUPS, tokens, gw), F32),
            pltpu.VMEM((GROUPS, state_dim, gw), F32),
            pltpu.VMEM((GROUPS, CUTS, state_dim, gw // CUTS), BF16),
            pltpu.VMEM((GROUPS, CUTS, state_dim, gw // CUTS), BF16),
            pltpu.VMEM((kv_count, HEAD_SIZE, qw), BF16),
            pltpu.VMEM((kv_count, HEAD_SIZE, qw), F32),
            pltpu.VMEM((kv_count, 1, qw), F32),
            pltpu.VMEM((kv_count, 1, qw), F32),
            dma((8,)),
            dma((n,)),
            dma((n,)),
            dma((n,)),
            dma((n,)),
            dma((GROUPS, CUTS)),
            dma((GROUPS, CUTS)),
        ],
        compiler_params=pltpu.CompilerParams(
            collective_id=0, has_side_effects=True, vmem_limit_bytes=56 * 1024 * 1024
        ),
    )(
        student_x, student_z, student_b, student_c, step_size, decay_rate[None, :],
        norm_gain[None, :], teacher_q, teacher_k, teacher_v,
    )
    results = [pltpu.with_memory_space_constraint(r, pltpu.VMEM) for r in results]
    return pl.pallas_call(
        store,
        out_shape=(
            jax.ShapeDtypeStruct(student_x.shape, BF16),
            jax.ShapeDtypeStruct(teacher_q.shape, BF16),
        ),
        in_specs=[vmem, vmem],
        out_specs=(hbm, hbm),
        scratch_shapes=[dma((2,))],
    )(*results)


def solution(mesh):
    return jax.shard_map(
        on_device,
        mesh=mesh,
        in_specs=(
            P(("dp", "seq"), None),
            P(("dp", "seq"), None),
            P(("dp", "seq"), None),
            P(("dp", "seq"), None),
            P(None, ("dp", "seq")),
            P(),
            P(),
            P(("dp", "seq"), None),
            P(("dp", "seq"), None),
            P(("dp", "seq"), None),
        ),
        out_specs=(P(("dp", "seq"), None), P(("dp", "seq"), None)),
        check_vma=False,
    )
```

```python
import functools
import math

import jax
import jax.numpy as jnp
from jax import lax
from jax.experimental import pallas as pl
from jax.experimental.pallas import tpu as pltpu
from jax.sharding import PartitionSpec as P

GROUPS = 8
HEAD_SIZE = 128
BLOCK = 128
CUTS = 1

epsilon_norm = 1e-05
masked_score = -1e30
F32 = jnp.float32
BF16 = jnp.bfloat16
MESH = pl.DeviceIdType.MESH


def dot(a, b, ca=1, cb=0):
    return lax.dot_general(a, b, (((ca,), (cb,)), ((), ())), preferred_element_type=F32)


def kernel(
    n,
    x_hbm, z_hbm, b_hbm, c_hbm, step_hbm, rate_ref, gain_ref, q_hbm, k_hbm, v_hbm,
    so_ref, to_ref,
    x_ref, z_ref, b_ref, c_ref, step_ref, q_ref, kbuf, vbuf,
    cum_ref, ssm_ref, reach_ref, stl_ref, stin_ref, stout_ref,
    qt_ref, acc_ref, max_ref, sum_ref,
    in_sem, k_send, k_recv, v_send, v_recv, s_send, s_recv,
):
    me = lax.axis_index("seq")
    right = lax.rem(me + 1, n)
    left = lax.rem(me + n - 1, n)
    has_left = me > 0
    has_right = me < n - 1
    tokens, width = x_ref.shape
    heads = step_ref.shape[0]
    per_group = heads // GROUPS
    head_width = width // heads
    gw = width // GROUPS
    state_dim = b_ref.shape[1] // GROUPS
    kv_count = k_hbm.shape[1] // HEAD_SIZE
    qw = q_ref.shape[1] // kv_count
    ratio = qw // HEAD_SIZE
    lanes = 128
    pack = lanes // head_width
    scale = math.log2(math.e) / math.sqrt(HEAD_SIZE)

    loads = [
        pltpu.make_async_copy(src, dst, in_sem.at[i])
        for i, (src, dst) in enumerate(
            (
                (step_hbm, step_ref), (q_hbm, q_ref), (k_hbm, kbuf.at[me]), (v_hbm, vbuf.at[me]),
                (b_hbm, b_ref), (c_hbm, c_ref), (x_hbm, x_ref), (z_hbm, z_ref),
            )
        )
    ]
    for load in loads:
        load.start()

    barrier = pltpu.get_barrier_semaphore()

    @pl.when(has_left)
    def _():
        pl.semaphore_signal(barrier, inc=1, device_id={"seq": left}, device_id_type=MESH)

    @pl.when(has_right)
    def _():
        pl.semaphore_signal(barrier, inc=1, device_id={"seq": right}, device_id_type=MESH)

    pl.semaphore_wait(barrier, has_left.astype(jnp.int32) + has_right.astype(jnp.int32))

    def key_copy(slot, source):
        return pltpu.make_async_remote_copy(
            src_ref=source, dst_ref=kbuf.at[slot], send_sem=k_send.at[slot],
            recv_sem=k_recv.at[slot], device_id={"seq": right}, device_id_type=MESH,
        )

    def value_copy(slot, source):
        return pltpu.make_async_remote_copy(
            src_ref=source, dst_ref=vbuf.at[slot], send_sem=v_send.at[slot],
            recv_sem=v_recv.at[slot], device_id={"seq": right}, device_id_type=MESH,
        )

    def state_copy(g, cut):
        return pltpu.make_async_remote_copy(
            src_ref=stout_ref.at[g, cut], dst_ref=stin_ref.at[g, cut], send_sem=s_send.at[g, cut],
            recv_sem=s_recv.at[g, cut], device_id={"seq": right}, device_id_type=MESH,
        )

    @pl.when(has_right)
    def _():
        for copy in (key_copy(me, k_hbm), value_copy(me, v_hbm)):
            copy.start()

    def span(g, size):
        return pl.ds(pl.multiple_of(g * size, 128), size)

    loads[0].wait()
    eye = lax.broadcasted_iota(jnp.int32, (heads, heads), 0) == lax.broadcasted_iota(
        jnp.int32, (heads, heads), 1
    )
    rate = jnp.sum(jnp.where(eye, rate_ref[...], 0.0), axis=1, keepdims=True)
    running = -step_ref[...] * rate
    position = lax.broadcasted_iota(jnp.int32, (heads, tokens), 1)
    shift = 1
    while shift < tokens:
        running = running + jnp.where(position >= shift, pltpu.roll(running, shift, 1), 0.0)
        shift *= 2
    cum_ref[...] = running

    key_at = lax.broadcasted_iota(jnp.int32, (tokens, tokens), 0)
    query_at = lax.broadcasted_iota(jnp.int32, (tokens, tokens), 1)
    half = lax.broadcasted_iota(jnp.int32, (tokens, lanes), 1) // head_width
    row_half = lax.broadcasted_iota(jnp.int32, (1, lanes), 1) // head_width
    pairs = per_group // pack
    cut_pairs = pairs // CUTS

    def columns_of(g, p):
        return pl.ds(pl.multiple_of(g * gw + p * lanes, 128), lanes)

    def relay_key(slot):
        copy = key_copy(slot, kbuf.at[slot])
        copy.wait_recv()

        @pl.when(has_right)
        def _():
            copy.start()

    def relay_value(slot):
        copy = value_copy(slot, vbuf.at[slot])
        copy.wait_recv()

        @pl.when(has_right)
        def _():
            copy.start()

    visible = jnp.concatenate([(key_at <= query_at).astype(F32)] * ratio, axis=1) > 0.5

    def attend_own(g):
        for h in range(ratio):
            piece = q_ref[:, pl.ds(pl.multiple_of(g * qw + h * HEAD_SIZE, 128), HEAD_SIZE)]
            qt_ref[g, :, h * HEAD_SIZE : (h + 1) * HEAD_SIZE] = piece.T
        scores = dot(kbuf[me, :, span(g, HEAD_SIZE)], qt_ref[g]) * scale
        scores = jnp.where(visible, scores, masked_score)
        top = jnp.max(scores, axis=0, keepdims=True)
        weight = jnp.exp2(scores - top)
        max_ref[g] = top
        sum_ref[g] = jnp.sum(weight, axis=0, keepdims=True)
        acc_ref[g] = dot(vbuf[me, :, span(g, HEAD_SIZE)], weight.astype(BF16), 0, 0)

    for load in loads[1:]:
        load.wait()
    lower = query_at <= key_at

    def student_local(g):
        cum = cum_ref[pl.ds(pl.multiple_of(g * per_group, 8), per_group), :]
        cum_t = cum.T
        tail = jnp.exp(cum[:, tokens - 1 : tokens] - cum)
        b = b_ref[:, span(g, state_dim)]
        b_t = b.T.astype(F32)
        products = dot(c_ref[:, span(g, state_dim)], b, 1, 1)
        for p in range(pairs):
            x = x_ref[:, columns_of(g, p)].astype(F32)
            mixes = []
            adds = []
            sources = []
            reach = None
            for j in range(pack):
                h = p * pack + j
                column = jnp.broadcast_to(cum_t[:, h : h + 1], (tokens, lanes))
                difference = jnp.where(lower, column - cum[h : h + 1, :], masked_score)
                mixes.append((products * jnp.exp(difference)).astype(BF16))
                adds.append((b_t * tail[h : h + 1, :]).astype(BF16))
                sources.append(jnp.where(half == j, x, 0.0).astype(BF16))
                reach = column if j == 0 else jnp.where(half == j, column, reach)
            z = z_ref[:, columns_of(g, p)].astype(F32)
            gate = z / (1.0 + jnp.exp(-z))
            at = slice(p * lanes, (p + 1) * lanes)
            source = jnp.concatenate(sources, axis=0)
            ssm_ref[g, :, at] = gate * dot(jnp.concatenate(mixes, axis=1), source)
            reach_ref[g, :, at] = gate * jnp.exp(reach)
            stl_ref[g, :, at] = dot(jnp.concatenate(adds, axis=1), source)

        @pl.when(me == 0)
        def _():
            for cut in range(CUTS):
                size = gw // CUTS
                stout_ref[g, cut] = stl_ref[g, :, cut * size : (cut + 1) * size].astype(BF16)
                stin_ref[g, cut] = jnp.zeros((state_dim, size), BF16)

    def attend(slot):
        @pl.loop(0, kv_count)
        def _(g):
            scores = dot(kbuf[slot, :, span(g, HEAD_SIZE)], qt_ref[g]) * scale
            old = max_ref[g]
            top = jnp.maximum(old, jnp.max(scores, axis=0, keepdims=True))
            shrink = jnp.exp2(old - top)
            weight = jnp.exp2(scores - top)
            max_ref[g] = top
            sum_ref[g] = sum_ref[g] * shrink + jnp.sum(weight, axis=0, keepdims=True)
            acc_ref[g] = acc_ref[g] * shrink + dot(
                vbuf[slot, :, span(g, HEAD_SIZE)], weight.astype(BF16), 0, 0
            )

    near = lax.rem(me, 2) == 1
    far = jnp.logical_not(near)
    pieces = 2 * me

    @pl.loop(0, GROUPS)
    def _(r):
        student_local(r)
        attend_own(r)
        piece = jnp.where(near, (r + 1) // 2, (r - 2) // 2)

        @pl.when(jnp.logical_and(near, r == 0))
        def _():
            relay_key(me - 1)
            relay_value(me - 1)

        turn = jnp.where(near, r - 3, r - 2)
        due = jnp.logical_and(turn >= 0, piece < pieces)

        @pl.when(jnp.logical_and(due, lax.rem(turn + 4, 4) == 0))
        def _():
            relay_key(me - 1 - piece // 2)

        @pl.when(jnp.logical_and(due, lax.rem(turn + 4, 4) == 2))
        def _():
            relay_value(me - 1 - piece // 2)

    @pl.when(jnp.logical_and(me == 0, has_right))
    def _():
        @pl.loop(0, GROUPS)
        def _(g):
            for cut in range(CUTS):
                state_copy(g, cut).start()

    first = jnp.where(near, GROUPS // 2 + 1, GROUPS // 2 - 1)

    @pl.loop(0, me)
    def _(j):
        attend(me - 1 - j)
        piece = first + 2 * j

        @pl.when(piece < pieces)
        def _():
            relay_value(me - 1 - piece // 2)

        @pl.when(piece + 1 < pieces)
        def _():
            relay_key(me - 1 - (piece + 1) // 2)

    @pl.loop(0, kv_count)
    def _(g):
        result = acc_ref[g] / sum_ref[g]
        for h in range(ratio):
            to_ref[:, pl.ds(pl.multiple_of(g * qw + h * HEAD_SIZE, 128), HEAD_SIZE)] = (
                result[:, h * HEAD_SIZE : (h + 1) * HEAD_SIZE].T.astype(BF16)
            )

    mean_of = jnp.where(
        lax.broadcasted_iota(jnp.int32, (lanes, lanes), 0) // head_width
        == lax.broadcasted_iota(jnp.int32, (lanes, lanes), 1) // head_width,
        1.0 / head_width,
        0.0,
    ).astype(BF16)

    @pl.loop(0, GROUPS)
    def _(g):
        cum = cum_ref[pl.ds(pl.multiple_of(g * per_group, 8), per_group), :]
        total = jnp.exp(cum[:, tokens - 1 : tokens])
        c = c_ref[:, span(g, state_dim)]
        for cut in range(CUTS):

            @pl.when(has_left)
            def _():
                state_copy(g, cut).wait_recv()

            state = stin_ref[g, cut]

            @pl.when(jnp.logical_and(has_left, has_right))
            def _():
                for i in range(cut_pairs):
                    p = cut * cut_pairs + i
                    at = slice(i * lanes, (i + 1) * lanes)
                    decay = total[p * pack : p * pack + 1, :]
                    for j in range(1, pack):
                        decay = jnp.where(
                            row_half == j, total[p * pack + j : p * pack + j + 1, :], decay
                        )
                    stout_ref[g, cut, :, at] = (
                        state[:, at].astype(F32) * decay
                        + stl_ref[g, :, p * lanes : (p + 1) * lanes]
                    ).astype(BF16)
                state_copy(g, cut).start()

            carried = dot(c, state)
            for i in range(cut_pairs):
                p = cut * cut_pairs + i
                at = slice(p * lanes, (p + 1) * lanes)
                gated = ssm_ref[g, :, at] + reach_ref[g, :, at] * carried[:, i * lanes : (i + 1) * lanes]
                mean = dot((gated * gated).astype(BF16), mean_of)
                so_ref[:, columns_of(g, p)] = (
                    gated * lax.rsqrt(mean + epsilon_norm) * gain_ref[:, columns_of(g, p)]
                ).astype(BF16)

    @pl.when(has_right)
    def _():
        @pl.loop(0, GROUPS)
        def _(g):
            for cut in range(CUTS):
                state_copy(g, cut).wait_send()

        for copy in (key_copy(me, k_hbm), value_copy(me, v_hbm)):
            copy.wait_send()

        @pl.loop(0, me)
        def _(slot):
            for copy in (key_copy(slot, kbuf.at[slot]), value_copy(slot, vbuf.at[slot])):
                copy.wait_send()


def store(s_ref, t_ref, s_out, t_out, sem):
    copies = [
        pltpu.make_async_copy(s_ref, s_out, sem.at[0]),
        pltpu.make_async_copy(t_ref, t_out, sem.at[1]),
    ]
    for copy in copies:
        copy.start()
    for copy in copies:
        copy.wait()


def on_device(
    student_x, student_z, student_b, student_c, step_size, decay_rate, norm_gain,
    teacher_q, teacher_k, teacher_v,
):
    n = lax.axis_size("seq")
    tokens, width = student_x.shape
    heads = step_size.shape[0]
    assert tokens == BLOCK
    gw = width // GROUPS
    state_dim = student_b.shape[1] // GROUPS
    kv_count = teacher_k.shape[1] // HEAD_SIZE
    qw = teacher_q.shape[1] // kv_count
    hbm = pl.BlockSpec(memory_space=pl.ANY)
    vmem = pl.BlockSpec(memory_space=pltpu.VMEM)
    dma = pltpu.SemaphoreType.DMA
    results = pl.pallas_call(
        functools.partial(kernel, n),
        out_shape=(
            pltpu.VMEM(student_x.shape, BF16),
            pltpu.VMEM(teacher_q.shape, BF16),
        ),
        in_specs=[hbm, hbm, hbm, hbm, hbm, vmem, vmem, hbm, hbm, hbm],
        out_specs=(vmem, vmem),
        scratch_shapes=[
            pltpu.VMEM(student_x.shape, BF16),
            pltpu.VMEM(student_z.shape, BF16),
            pltpu.VMEM(student_b.shape, BF16),
            pltpu.VMEM(student_c.shape, BF16),
            pltpu.VMEM(step_size.shape, F32),
            pltpu.VMEM(teacher_q.shape, BF16),
            pltpu.VMEM((n,) + teacher_k.shape, BF16),
            pltpu.VMEM((n,) + teacher_v.shape, BF16),
            pltpu.VMEM(step_size.shape, F32),
            pltpu.VMEM((GROUPS, tokens, gw), F32),
            pltpu.VMEM((GROUPS, tokens, gw), F32),
            pltpu.VMEM((GROUPS, state_dim, gw), F32),
            pltpu.VMEM((GROUPS, CUTS, state_dim, gw // CUTS), BF16),
            pltpu.VMEM((GROUPS, CUTS, state_dim, gw // CUTS), BF16),
            pltpu.VMEM((kv_count, HEAD_SIZE, qw), BF16),
            pltpu.VMEM((kv_count, HEAD_SIZE, qw), F32),
            pltpu.VMEM((kv_count, 1, qw), F32),
            pltpu.VMEM((kv_count, 1, qw), F32),
            dma((8,)),
            dma((n,)),
            dma((n,)),
            dma((n,)),
            dma((n,)),
            dma((GROUPS, CUTS)),
            dma((GROUPS, CUTS)),
        ],
        compiler_params=pltpu.CompilerParams(
            collective_id=0, has_side_effects=True, vmem_limit_bytes=56 * 1024 * 1024
        ),
    )(
        student_x, student_z, student_b, student_c, step_size, decay_rate[None, :],
        norm_gain[None, :], teacher_q, teacher_k, teacher_v,
    )
    results = [pltpu.with_memory_space_constraint(r, pltpu.VMEM) for r in results]
    return pl.pallas_call(
        store,
        out_shape=(
            jax.ShapeDtypeStruct(student_x.shape, BF16),
            jax.ShapeDtypeStruct(teacher_q.shape, BF16),
        ),
        in_specs=[vmem, vmem],
        out_specs=(hbm, hbm),
        scratch_shapes=[dma((2,))],
    )(*results)


def solution(mesh):
    return jax.shard_map(
        on_device,
        mesh=mesh,
        in_specs=(
            P(("dp", "seq"), None),
            P(("dp", "seq"), None),
            P(("dp", "seq"), None),
            P(("dp", "seq"), None),
            P(None, ("dp", "seq")),
            P(),
            P(),
            P(("dp", "seq"), None),
            P(("dp", "seq"), None),
            P(("dp", "seq"), None),
        ),
        out_specs=(P(("dp", "seq"), None), P(("dp", "seq"), None)),
        check_vma=False,
    )
```
